32 devices in a mesh: groups: 2 (over x), ctx: 16 (over z, y, core).
Axes of the slice: x: 2, y: 2, z: 4, core: 2. Of those that a mesh axis runs over, the one named last changes fastest.
Arguments:
- queries: bfloat16 [12288, 2048], P(('groups', 'ctx')), parts along dimension 0, may hold values from -9 to 9
- key_vectors: bfloat16 [12288, 512], P(('groups', 'ctx')), parts along dimension 0, may hold values from -9 to 9
- values: bfloat16 [12288, 512], P(('groups', 'ctx')), parts along dimension 0, may hold values from -6 to 6
- frame_length: int32 [32], P('groups'), parts along dimension 0, may hold values from 2 to 6, as said below
- frame_reach: int32 [32], P('groups'), parts along dimension 0, may hold values from 0 to 11, as said below
- out_gain: float32 [2048], replicated, may hold values from 0.1 to 1.9
Outputs:
- normed: bfloat16 [12288, 2048], P(('groups', 'ctx')), parts along dimension 0
The draws below stay inside these ranges and needn't reach their ends.
There are 2 independent parts, one for each index of `groups`. The reference program is written for one: setup_inputs(seed, part) draws one part's arguments, and reference() takes and returns one part's arrays. A program takes and returns all parts, laid end to end along the dimension named above; an argument that names none is the same for every part. Nothing has to cross between parts.
Inputs may be any that keep to these rules, and one draw needn't show every extreme that they name: `frame_length`: frame 0 has length 2 and the last frame length 6; frames 1 and 2, 3 and 4, and so on come in consecutive pairs whose lengths add up to 8, the first of each pair of length 5 or 6. `frame_reach`: some frame 2q + 1 with q >= 2 has reach 11.
All inputs are finite; a program needn't handle non-finite values.
Results may differ from the reference program's by a relative error of at most 0.0055.
Values may be sent and summed in bfloat16 or wider, within the bound.
A program may use at most 128 MiB of HBM per device.

```python
import jax
import jax.numpy as jnp
from jax import lax

KV_HEADS = 4
HD = 128
GROUP = 4
DQ = 2048
DKV = 512
CH = 96
CTXMAX = 11
NCHUNK = 64
FRAMES = 16
S = 6144


def paired_vectors(key):
    base = jax.random.fold_in(key, 11)
    query_key, keyrow_key = jax.random.split(base, 2)
    query_part = jnp.clip(1.5 * jax.random.normal(query_key, (S, DQ), jnp.float32), -6.0, 6.0)
    key_part = jnp.clip(jax.random.normal(keyrow_key, (S, DKV), jnp.float32), -6.0, 6.0)
    return (query_part, key_part)


def draw_queries(key, part):
    query_part, key_part = paired_vectors(key)
    return query_part.astype(jnp.bfloat16)


def draw_key_vectors(key, part):
    query_part, key_part = paired_vectors(key)
    return key_part.astype(jnp.bfloat16)


def frame_plan(key):
    base = jax.random.fold_in(key, 23)
    length_key, reach_key, pick_key = jax.random.split(base, 3)
    pair_count = (FRAMES - 2) // 2
    leading = jax.random.randint(length_key, (pair_count,), 5, 7, dtype=jnp.int32)
    chosen_pair = jax.random.randint(pick_key, (), 2, pair_count, dtype=jnp.int32)
    middle = jnp.stack([leading, 8 - leading], axis=1).reshape(FRAMES - 2).astype(jnp.int32)
    lengths = jnp.concatenate([jnp.full((1,), 2, jnp.int32), middle, jnp.full((1,), 6, jnp.int32)]).astype(jnp.int32)
    reach = jax.random.randint(reach_key, (FRAMES,), 0, CTXMAX + 1, dtype=jnp.int32)
    reach = jnp.where(jnp.arange(FRAMES, dtype=jnp.int32) == 2 * chosen_pair + 1, CTXMAX, reach).astype(jnp.int32)
    return (lengths, reach)


def draw_frame_length(key, part):
    lengths, reach = frame_plan(key)
    return lengths


def draw_frame_reach(key, part):
    lengths, reach = frame_plan(key)
    return reach


def shard_levels(key, dims, cuts, least, largest):
    def one(dim, blocks):
        draws = jax.random.uniform(jax.random.fold_in(jax.random.fold_in(key, 6), dim), (blocks,), jnp.float32, least / len(cuts), largest / len(cuts))
        return jnp.repeat(jnp.exp(draws), dims[dim] // blocks).reshape((-1,) + (1,) * (len(dims) - dim - 1))

    loudness = one(*cuts[0])
    for cut in cuts[1:]:
        loudness = loudness * one(*cut)
    return loudness


def gaussian(key, extent, deviation, limit, cuts=(), kind=jnp.bfloat16):
    values = deviation * jax.random.normal(key, extent, jnp.float32)
    if cuts:
        values = values * shard_levels(key, extent, cuts, -0.22, 0.18)
    return jnp.clip(values, -limit, limit).astype(kind)


def setup_inputs(seed: int = 0, part: int = 0) -> dict:
    splits = jax.random.split(jax.random.key(seed), 7)
    part_keys = jax.random.split(jax.random.fold_in(splits[6], part), 7)
    return {
        "queries": draw_queries(jax.random.fold_in(jax.random.fold_in(splits[6], part), 71), part),
        "key_vectors": draw_key_vectors(jax.random.fold_in(jax.random.fold_in(splits[6], part), 71), part),
        "values": gaussian(part_keys[2], (S, DKV), 1.0, 6.0, ((0, 16),)),
        "frame_length": draw_frame_length(jax.random.fold_in(jax.random.fold_in(splits[6], part), 71), part),
        "frame_reach": draw_frame_reach(jax.random.fold_in(jax.random.fold_in(splits[6], part), 71), part),
        "out_gain": jnp.clip(1.0 + 0.18 * jax.random.normal(splits[5], (DQ,), jnp.float32), 0.1, 1.9),
    }


def block_ranges(frame_length, frame_reach):
    ends = jnp.cumsum(frame_length).astype(jnp.int32)
    starts = (ends - frame_length).astype(jnp.int32)
    count = 4 * frame_length.shape[0]
    block_ids = jnp.arange(count, dtype=jnp.int32)
    inside = ((block_ids[:, None] >= starts[None, :]) & (block_ids[:, None] < ends[None, :])).astype(jnp.int32)
    earliest = jnp.maximum(starts - frame_reach, 0).astype(jnp.int32)
    lower = lax.optimization_barrier(jnp.sum(inside * earliest[None, :], axis=1)).astype(jnp.int32)
    upper = lax.optimization_barrier(jnp.sum(inside * ends[None, :], axis=1)).astype(jnp.int32)
    return (lower, upper)

def reference(queries, key_vectors, values, frame_length, frame_reach, out_gain):
    lower, upper = block_ranges(frame_length, frame_reach)
    reach_back = 5 + CTXMAX
    window = (reach_back + 6) * CH
    padded_keys = jnp.pad(key_vectors, ((reach_back * CH, 6 * CH), (0, 0)))
    padded_values = jnp.pad(values, ((reach_back * CH, 6 * CH), (0, 0)))
    scale = 1.0 / HD ** 0.5

    def one_block(block_id):
        query_rows = lax.dynamic_slice_in_dim(queries, block_id * CH, CH, 0).astype(jnp.float32)
        query_rows = query_rows.reshape(CH, KV_HEADS, GROUP, HD)
        key_rows = lax.dynamic_slice_in_dim(padded_keys, block_id * CH, window, 0).astype(jnp.float32)
        key_rows = key_rows.reshape(window, KV_HEADS, HD)
        value_rows = lax.dynamic_slice_in_dim(padded_values, block_id * CH, window, 0).astype(jnp.float32)
        value_rows = value_rows.reshape(window, KV_HEADS, HD)
        scores = jnp.einsum('qghd,kgd->qghk', query_rows, key_rows, precision=lax.Precision.HIGHEST) * scale
        positions = (block_id - reach_back) * CH + jnp.arange(window, dtype=jnp.int32)
        allowed = (positions >= lower[block_id] * CH) & (positions < upper[block_id] * CH)
        masked = jnp.where(allowed, scores, jnp.float32(-1e+30))
        row_max = lax.optimization_barrier(jnp.max(masked, axis=-1, keepdims=True))
        weights = jnp.where(allowed, jnp.exp(masked - row_max), jnp.float32(0.0)).astype(jnp.bfloat16)
        weights_wide = weights.astype(jnp.float32)
        totals = lax.optimization_barrier(jnp.sum(weights_wide, axis=-1))
        numerator = jnp.einsum('qghk,kgd->qghd', weights_wide, value_rows, precision=lax.Precision.HIGHEST)
        attended = (numerator / totals[..., None]).reshape(CH, DQ)
        mean_square = lax.optimization_barrier(jnp.mean(attended * attended, axis=-1, keepdims=True))
        return (attended * lax.rsqrt(mean_square + 1e-06) * out_gain).astype(jnp.bfloat16)
    result = lax.map(one_block, jnp.arange(NCHUNK, dtype=jnp.int32))
    return result.reshape(S, DQ)
```

```python
import functools

import jax
import jax.numpy as jnp
from jax import lax
from jax.experimental import pallas as pl
from jax.experimental.pallas import tpu as pltpu
from jax.sharding import PartitionSpec as P

HD = 128
MESH = pl.DeviceIdType.MESH
BACK = 12
SPAN = 22
WIDE = 17
CHUNK = 256


def kernel(
    n, block, kv_heads, group,
    q_hbm, k_hbm, v_hbm, len_ref, reach_ref, gain_ref,
    o_ref,
    kv, qv, s_even, s_odd, att, lo_ref, up_ref,
    local_sem, q_sem, send_sem, recv_sem,
):
    me = lax.axis_index("ctx")
    chip = lax.div(me, 2)
    core = lax.rem(me, 2)
    chips = n // 2
    mate = 2 * chip + 1 - core
    tokens = 4 * block
    rows = group * block

    has_next = chip < chips - 1
    has_prev = chip > 0
    has_far_next = jnp.logical_and(core == 1, chip < chips - 2)
    has_far_prev = jnp.logical_and(core == 0, chip > 1)
    gives_back = jnp.logical_and(core == 0, has_prev)
    gets_back = jnp.logical_and(core == 1, has_next)
    odd = lax.rem(chip, 2) == 1
    skips = jnp.logical_and(odd, core == 1)
    gives_near = jnp.logical_and(has_next, jnp.logical_not(skips))
    gets_relay = jnp.logical_and(has_prev, jnp.logical_and(jnp.logical_not(odd), core == 1))
    gets_near = jnp.logical_and(has_prev, jnp.logical_not(gets_relay))
    relays = jnp.logical_and(has_far_prev, odd)

    def span(start, count):
        if isinstance(start, int):
            return pl.ds(start * block, count * block)
        return pl.ds(pl.multiple_of(start * block, 32), count * block)

    own = span(BACK + 4 * core, 4)

    for g in range(kv_heads):
        cols = pl.ds(g * HD, HD)
        pltpu.make_async_copy(k_hbm.at[:, cols], kv.at[g, 0, own, :], local_sem.at[g, 0]).start()
        pltpu.make_async_copy(v_hbm.at[:, cols], kv.at[g, 1, own, :], local_sem.at[g, 1]).start()
    q_copy = pltpu.make_async_copy(q_hbm, qv, q_sem)
    q_copy.start()

    barrier = pltpu.get_barrier_semaphore()

    def greet(cond, target):
        @pl.when(cond)
        def _():
            pl.semaphore_signal(barrier, inc=1, device_id={"ctx": target}, device_id_type=MESH)

        return cond.astype(jnp.int32)

    pl.semaphore_signal(barrier, inc=1, device_id={"ctx": mate}, device_id_type=MESH)
    expected = jnp.int32(1)
    expected += greet(has_next, me + 2)
    expected += greet(has_prev, me - 2)
    expected += greet(has_far_next, me + 3)
    expected += greet(has_far_prev, me - 3)
    expected += greet(gives_back, me - 1)
    expected += greet(gets_back, me + 1)

    def clear(cond, first, count):
        @pl.when(cond)
        def _():
            kv[:, :, first * block : (first + count) * block, :] = jnp.zeros(
                (kv_heads, 2, count * block, HD), jnp.bfloat16
            )

    clear(chip == 0, 0, 12)
    clear(chip == 1, 0, 4)
    clear(jnp.logical_and(core == 1, chip > 1), 0, 3)
    clear(jnp.logical_or(core == 0, chip == chips - 1), 20, 2)

    pl.semaphore_wait(barrier, expected)

    def copy(g, kind, target, source, dest):
        return pltpu.make_async_remote_copy(
            src_ref=kv.at[g, :, source, :],
            dst_ref=kv.at[g, :, dest, :],
            send_sem=send_sem.at[g, kind],
            recv_sem=recv_sem.at[g, kind],
            device_id={"ctx": target},
            device_id_type=MESH,
        )

    near = span(4 + 4 * core, 4)

    def to_next(g):
        return copy(g, 0, me + 2, own, near)

    def to_far(g):
        return copy(g, 1, me + 3, own, span(0, 4))

    def to_back(g):
        return copy(g, 2, me - 1, span(BACK, 2), span(20, 2))

    def relay(g):
        return copy(g, 6, me - 1, span(0, 4), span(8, 4))

    def to_mate(g):
        return copy(g, 3, mate, own, own)

    def near_to_mate(g):
        return copy(g, 4, mate, near, near)

    def far_to_mate(g):
        return copy(g, 5, mate, span(3, 1), span(3, 1))

    def from_mate(g):
        theirs = span(BACK + 4 - 4 * core, 4)
        return copy(g, 3, mate, theirs, theirs)

    def near_from_mate(g):
        theirs = span(8 - 4 * core, 4)
        return copy(g, 4, mate, theirs, theirs)

    for g in range(kv_heads):
        cols = pl.ds(g * HD, HD)
        pltpu.make_async_copy(k_hbm.at[:, cols], kv.at[g, 0, own, :], local_sem.at[g, 0]).wait()
        pltpu.make_async_copy(v_hbm.at[:, cols], kv.at[g, 1, own, :], local_sem.at[g, 1]).wait()
        pl.when(has_far_next)(lambda g=g: to_far(g).start())
        pl.when(gives_near)(lambda g=g: to_next(g).start())
        pl.when(gives_back)(lambda g=g: to_back(g).start())
        to_mate(g).start()

    first = 8 * chip - BACK

    def ranges(f, carry):
        start = carry[0]
        end = start + len_ref[f]
        low = jnp.maximum(start - reach_ref[f], 0)
        lows, highs = [], []
        for r in range(4):
            c = 4 * me + r
            inside = jnp.logical_and(c >= start, c < end)
            lows.append(jnp.where(inside, low, carry[1][r]))
            highs.append(jnp.where(inside, end, carry[2][r]))
        return end, tuple(lows), tuple(highs)

    zero = jnp.int32(0)
    _, lows, highs = lax.fori_loop(
        0, len_ref.shape[0], ranges, (zero, (zero,) * 4, (zero,) * 4)
    )
    for r in range(4):
        lo_ref[r] = lows[r] - first
        up_ref[r] = highs[r] - first

    factor = 1.4426950408889634 / HD**0.5
    q_copy.wait()

    def rows_from(start, count):
        return pl.ds(start if isinstance(start, int) else pl.multiple_of(start, 32), count)

    tall = WIDE * block
    cuts = list(range(0, tall, CHUNK)) + [tall]
    pieces = []
    for top, end in zip(cuts[:-1], cuts[1:]):
        edges = [top] + [b for b in range(0, tall, block) if top < b < end] + [end]
        pieces.append((top, end, [(a, b, a // block) for a, b in zip(edges[:-1], edges[1:])]))

    def fold(x, op):
        return op(x.reshape(x.shape[0] // 8, 8, rows), axis=0)

    def prepare(g, r):
        low = lo_ref[r]
        up = up_ref[r]
        w0 = 3 if r > 1 else 3 * core
        swap = up > w0 + WIDE
        places = [jnp.where(swap, SPAN - 2 + j, w0 + j) for j in range(2)]
        places += [w0 + j for j in range(2, WIDE)]
        kept = [jnp.logical_and(place >= low, place < up) for place in places]

        def load(half, top, end):
            if top >= 2 * block or r < 3:
                return kv[g, half, rows_from(w0 * block + top, end - top), :]
            ends = jnp.where(
                swap, kv[g, half, span(SPAN - 2, 2), :], kv[g, half, span(w0, 2), :]
            )
            rest = kv[g, half, rows_from((w0 + 2) * block, end - 2 * block), :]
            return jnp.concatenate([ends, rest], axis=0)

        qs = jnp.concatenate(
            [
                qv[r * block : (r + 1) * block, pl.ds(pl.multiple_of((group * g + h) * HD, HD), HD)]
                for h in range(group)
            ],
            axis=0,
        )
        state = {"best": jnp.full((8, rows), -1e30, jnp.float32), "kept": kept, "load": load, "qs": qs}
        state["scores"] = (s_even, s_odd)[r % 2]
        return state

    def score(state, top, end, parts):
        s = lax.dot_general(
            state["load"](0, top, end), state["qs"], (((1,), (1,)), ((), ())),
            preferred_element_type=jnp.float32,
        )
        state["scores"][top:end, :] = s
        for a, b, j in parts:
            peak = fold(s[a - top : b - top], jnp.max)
            state["best"] = jnp.maximum(
                state["best"], jnp.where(state["kept"][j], peak, jnp.float32(-1e30))
            )

    def close(state):
        best = jnp.max(state["best"], axis=0, keepdims=True) * factor
        state["shifts"] = [jnp.where(k, best, jnp.float32(1e30)) for k in state["kept"]]
        state["total"] = jnp.zeros((8, rows), jnp.float32)
        state["out"] = jnp.zeros((HD, rows), jnp.float32)

    def weigh(state, top, end, parts):
        weights = []
        for a, b, j in parts:
            p = jnp.exp2(state["scores"][a:b, :] * factor - state["shifts"][j])
            state["total"] += fold(p, jnp.sum)
            weights.append(p.astype(jnp.bfloat16))
        state["out"] += lax.dot_general(
            state["load"](1, top, end), jnp.concatenate(weights, axis=0), (((0,), (0,)), ((), ())),
            preferred_element_type=jnp.float32,
        )

    def finish(state, g, r):
        total = jnp.sum(state["total"], axis=0, keepdims=True)
        out = (state["out"] / total).T
        for h in range(group):
            att[r * block : (r + 1) * block, pl.ds(pl.multiple_of((group * g + h) * HD, HD), HD)] = (
                out[h * block : (h + 1) * block]
            )

    def head(g):
        state = prepare(g, 0)
        for piece in pieces:
            score(state, *piece)
        for r in range(4):
            close(state)
            later = prepare(g, r + 1) if r < 3 else None
            for piece in pieces:
                weigh(state, *piece)
                if later:
                    score(later, *piece)
            finish(state, g, r)
            if r == 1:
                pl.when(g < kv_heads - 1)(lambda: near_stage(g + 1))
            state = later

    def near_stage(g):
        @pl.when(gets_near)
        def _():
            copy(g, 0, me, near, near).wait_recv()
            near_to_mate(g).start()

        @pl.when(gets_relay)
        def _():
            relay(g).wait_recv()
            near_to_mate(g).start()

    def far_stage(g):
        @pl.when(has_far_prev)
        def _():
            copy(g, 1, me, span(0, 4), span(0, 4)).wait_recv()
            far_to_mate(g).start()

        @pl.when(relays)
        def _():
            relay(g).start()

    far_stage(0)
    near_stage(0)

    @pl.loop(0, kv_heads)
    def _(g):
        @pl.when(g < kv_heads - 1)
        def _():
            far_stage(g + 1)

        from_mate(g).wait_recv()

        @pl.when(gets_back)
        def _():
            copy(g, 2, me, span(20, 2), span(20, 2)).wait_recv()

        @pl.when(has_prev)
        def _():
            near_from_mate(g).wait_recv()

        @pl.when(jnp.logical_and(core == 1, chip > 1))
        def _():
            far_to_mate(g).wait_recv()

        head(g)

    @pl.loop(0, 4)
    def _(r):
        row = pl.ds(pl.multiple_of(r * block, 32), block)
        x = att[row, :]
        mean_square = jnp.mean(x * x, axis=-1, keepdims=True)
        o_ref[row, :] = (x * lax.rsqrt(mean_square + 1e-6) * gain_ref[...]).astype(jnp.bfloat16)

    for g in range(kv_heads):
        pl.when(gives_near)(lambda g=g: to_next(g).wait_send())
        pl.when(relays)(lambda g=g: relay(g).wait_send())
        pl.when(has_far_next)(lambda g=g: to_far(g).wait_send())
        pl.when(gives_back)(lambda g=g: to_back(g).wait_send())
        to_mate(g).wait_send()
        pl.when(has_prev)(lambda g=g: near_to_mate(g).wait_send())
        pl.when(has_far_prev)(lambda g=g: far_to_mate(g).wait_send())


def on_device(n, queries, key_vectors, values, frame_length, frame_reach, out_gain):
    tokens, width = queries.shape
    block = tokens // 4
    kv_heads = key_vectors.shape[1] // HD
    group = width // key_vectors.shape[1]
    anywhere = pl.BlockSpec(memory_space=pl.ANY)
    scalar = pl.BlockSpec(memory_space=pltpu.SMEM)
    return pl.pallas_call(
        functools.partial(kernel, n, block, kv_heads, group),
        out_shape=pltpu.VMEM((tokens, width), jnp.bfloat16),
        in_specs=[anywhere] * 3 + [scalar] * 2 + [pl.BlockSpec(memory_space=pltpu.VMEM)],
        out_specs=pl.BlockSpec(memory_space=pltpu.VMEM),
        scratch_shapes=[
            pltpu.VMEM((kv_heads, 2, SPAN * block, HD), jnp.bfloat16),
            pltpu.VMEM((tokens, width), jnp.bfloat16),
            pltpu.VMEM((WIDE * block, group * block), jnp.float32),
            pltpu.VMEM((WIDE * block, group * block), jnp.float32),
            pltpu.VMEM((tokens, width), jnp.float32),
            pltpu.SMEM((4,), jnp.int32),
            pltpu.SMEM((4,), jnp.int32),
            pltpu.SemaphoreType.DMA((kv_heads, 2)),
            pltpu.SemaphoreType.DMA,
            pltpu.SemaphoreType.DMA((kv_heads, 7)),
            pltpu.SemaphoreType.DMA((kv_heads, 7)),
        ],
        compiler_params=pltpu.CompilerParams(
            collective_id=0, has_side_effects=True, vmem_limit_bytes=60 * 1024 * 1024
        ),
    )(queries, key_vectors, values, frame_length, frame_reach, out_gain.reshape(1, width))


def solution(mesh):
    placed = (
        P(("groups", "ctx"), None),
        P(("groups", "ctx"), None),
        P(("groups", "ctx"), None),
        P("groups"),
        P("groups"),
        P(),
    )
    return jax.shard_map(
        functools.partial(on_device, mesh.shape["ctx"]),
        mesh=mesh, in_specs=placed, out_specs=P(("groups", "ctx"), None), check_vma=False,
    )
```

```python
import functools

import jax
import jax.numpy as jnp
from jax import lax
from jax.experimental import pallas as pl
from jax.experimental.pallas import tpu as pltpu
from jax.sharding import PartitionSpec as P

HD = 128
MESH = pl.DeviceIdType.MESH
BACK = 12
SPAN = 22
CHUNK = 256
EARLY = 2


def kernel(
    n, block, kv_heads, group,
    q_hbm, k_hbm, v_hbm, len_ref, reach_ref, gain_ref,
    o_ref,
    kv, qv, s_even, s_odd, att, acc, peaks, sums, lo_ref, up_ref,
    local_sem, q_sem, send_sem, recv_sem,
):
    me = lax.axis_index("ctx")
    chip = lax.div(me, 2)
    core = lax.rem(me, 2)
    chips = n // 2
    mate = 2 * chip + 1 - core
    tokens = 4 * block
    rows = group * block

    has_next = chip < chips - 1
    has_prev = chip > 0
    has_far_next = jnp.logical_and(core == 0, chip < chips - 2)
    has_far_prev = jnp.logical_and(core == 0, chip > 1)
    gives_back = jnp.logical_and(core == 0, has_prev)
    gets_back = jnp.logical_and(core == 1, has_next)
    odd = lax.rem(chip, 2) == 1
    skips = jnp.logical_and(odd, core == 1)
    gets_relay = jnp.logical_and(has_prev, jnp.logical_and(jnp.logical_not(odd), core == 1))
    relays = jnp.logical_and(has_far_prev, odd)
    even = jnp.logical_not(odd)

    def gives_near(g):
        return jnp.logical_and(has_next, jnp.logical_not(jnp.logical_and(skips, g > 0)))

    def relayed(g):
        return jnp.logical_and(gets_relay, g > 0)

    def direct(g):
        return jnp.logical_and(has_prev, jnp.logical_not(relayed(g)))

    def relaying(g):
        return jnp.logical_and(relays, g > 0)

    def span(start, count):
        if isinstance(start, int):
            return pl.ds(start * block, count * block)
        return pl.ds(pl.multiple_of(start * block, 32), count * block)

    own = span(BACK + 4 * core, 4)

    for g in range(kv_heads):
        cols = pl.ds(g * HD, HD)
        pltpu.make_async_copy(k_hbm.at[:, cols], kv.at[g, 0, own, :], local_sem.at[g, 0]).start()
        pltpu.make_async_copy(v_hbm.at[:, cols], kv.at[g, 1, own, :], local_sem.at[g, 1]).start()
    q_copy = pltpu.make_async_copy(q_hbm, qv, q_sem)
    q_copy.start()

    barrier = pltpu.get_barrier_semaphore()

    def greet(cond, target):
        @pl.when(cond)
        def _():
            pl.semaphore_signal(barrier, inc=1, device_id={"ctx": target}, device_id_type=MESH)

        return cond.astype(jnp.int32)

    pl.semaphore_signal(barrier, inc=1, device_id={"ctx": mate}, device_id_type=MESH)
    expected = jnp.int32(1)
    expected += greet(has_next, me + 2)
    expected += greet(has_prev, me - 2)
    expected += greet(has_far_next, me + 4)
    expected += greet(has_far_prev, me - 4)
    expected += greet(gives_back, me - 1)
    expected += greet(gets_back, me + 1)

    def clear(cond, first, count):
        @pl.when(cond)
        def _():
            kv[:, :, first * block : (first + count) * block, :] = jnp.zeros(
                (kv_heads, 2, count * block, HD), jnp.bfloat16
            )

    clear(chip == 0, 0, 12)
    clear(chip == 1, 0, 4)

    pl.semaphore_wait(barrier, expected)

    def copy(g, kind, target, source, dest):
        return pltpu.make_async_remote_copy(
            src_ref=kv.at[g, :, source, :],
            dst_ref=kv.at[g, :, dest, :],
            send_sem=send_sem.at[g, kind],
            recv_sem=recv_sem.at[g, kind],
            device_id={"ctx": target},
            device_id_type=MESH,
        )

    near = span(4 + 4 * core, 4)

    def to_next(g):
        return copy(g, 0, me + 2, own, near)

    def to_far(g):
        return copy(g, 1, me + 4, span(BACK + 4, 4), span(0, 4))

    def to_back(g):
        return copy(g, 2, me - 1, span(BACK, 2), span(20, 2))

    def relay(g):
        return copy(g, 6, me - 1, span(0, 4), span(8, 4))

    def to_mate(g):
        return copy(g, 3, mate, own, own)

    def near_to_mate(g):
        return copy(g, 4, mate, near, near)

    def far_to_mate(g):
        return copy(g, 5, mate, span(3, 1), span(3, 1))

    def from_mate(g):
        theirs = span(BACK + 4 - 4 * core, 4)
        return copy(g, 3, mate, theirs, theirs)

    def near_from_mate(g):
        theirs = span(8 - 4 * core, 4)
        return copy(g, 4, mate, theirs, theirs)

    for g in range(kv_heads):
        cols = pl.ds(g * HD, HD)
        pltpu.make_async_copy(k_hbm.at[:, cols], kv.at[g, 0, own, :], local_sem.at[g, 0]).wait()
        pltpu.make_async_copy(v_hbm.at[:, cols], kv.at[g, 1, own, :], local_sem.at[g, 1]).wait()
        next_now = odd if g == 0 else even
        pl.when(jnp.logical_and(gives_near(g), next_now))(lambda g=g: to_next(g).start())
        to_mate(g).start()
        if g < EARLY:
            pl.when(jnp.logical_and(gives_back, odd))(lambda g=g: to_back(g).start())
    pl.when(jnp.logical_and(gives_near(0), even))(lambda: to_next(0).start())

    first = 8 * chip - BACK

    def ranges(f, carry):
        start = carry[0]
        end = start + len_ref[f]
        low = jnp.maximum(start - reach_ref[f], 0)
        lows, highs = [], []
        for r in range(4):
            c = 4 * me + r
            inside = jnp.logical_and(c >= start, c < end)
            lows.append(jnp.where(inside, low, carry[1][r]))
            highs.append(jnp.where(inside, end, carry[2][r]))
        return end, tuple(lows), tuple(highs)

    zero = jnp.int32(0)
    _, lows, highs = lax.fori_loop(
        0, len_ref.shape[0], ranges, (zero, (zero,) * 4, (zero,) * 4)
    )
    for r in range(4):
        lo_ref[r] = lows[r] - first
        up_ref[r] = highs[r] - first

    factor = 1.4426950408889634 / HD**0.5
    q_copy.wait()

    def fold(x, op):
        return op(x.reshape(x.shape[0] // 8, 8, rows), axis=0)

    def cut(runs):
        places = [start + j for start, count in runs for j in range(count)]
        tall = len(places) * block
        pieces = []
        for top in range(0, tall, CHUNK):
            end = min(top + CHUNK, tall)
            edges = [top] + [b for b in range(0, tall, block) if top < b < end] + [end]
            loads, begin = [], 0
            for start, count in runs:
                a, b = max(top, begin), min(end, begin + count * block)
                if a < b:
                    loads.append((start, a - begin, b - a))
                begin += count * block
            pieces.append((top, end, [(a, b, a // block) for a, b in zip(edges[:-1], edges[1:])], loads))
        return places, pieces

    def own_runs(r):
        return [(BACK, 5)] if r < 2 else [(BACK, 8)]

    def earlier_runs(r):
        return ([((BACK + 5) * core, 3)] if r < 2 else []) + [(3, 9)]

    def prepare(g, r, runs, scores):
        places, pieces = cut(runs)
        low = lo_ref[r]
        up = up_ref[r]

        def load(half, loads):
            found = []
            for start, skip, count in loads:
                where = start * block + skip
                if not isinstance(start, int):
                    where = pl.multiple_of(where, 32)
                found.append(kv[g, half, pl.ds(where, count), :])
            return found[0] if len(found) == 1 else jnp.concatenate(found, axis=0)

        qs = jnp.concatenate(
            [
                qv[r * block : (r + 1) * block, pl.ds(pl.multiple_of((group * g + h) * HD, HD), HD)]
                for h in range(group)
            ],
            axis=0,
        )
        return {
            "best": jnp.full((8, rows), -1e30, jnp.float32),
            "kept": [jnp.logical_and(place >= low, place < up) for place in places],
            "pieces": pieces, "load": load, "qs": qs, "scores": scores,
            "slot": 4 * g + r, "g": g, "r": r,
        }

    def score(state, top, end, parts, loads):
        s = lax.dot_general(
            state["load"](0, loads), state["qs"], (((1,), (1,)), ((), ())),
            preferred_element_type=jnp.float32,
        )
        state["scores"][top:end, :] = s
        for a, b, j in parts:
            peak = fold(s[a - top : b - top], jnp.max)
            state["best"] = jnp.maximum(
                state["best"], jnp.where(state["kept"][j], peak, jnp.float32(-1e30))
            )

    def close(state, again):
        best = jnp.max(state["best"], axis=0, keepdims=True) * factor
        if again:
            before = peaks[state["slot"], :, :]
            best = jnp.maximum(best, before)
            state["fade"] = jnp.exp2(before - best)
        state["peak"] = best
        state["shifts"] = [jnp.where(k, best, jnp.float32(1e30)) for k in state["kept"]]
        state["total"] = jnp.zeros((8, rows), jnp.float32)
        state["out"] = jnp.zeros((HD, rows), jnp.float32)

    def weigh(state, top, end, parts, loads):
        weights = []
        for a, b, j in parts:
            p = jnp.exp2(state["scores"][a:b, :] * factor - state["shifts"][j])
            state["total"] += fold(p, jnp.sum)
            weights.append(p.astype(jnp.bfloat16))
        state["out"] += lax.dot_general(
            state["load"](1, loads), jnp.concatenate(weights, axis=0), (((0,), (0,)), ((), ())),
            preferred_element_type=jnp.float32,
        )

    def finish(state, again, keep, write):
        slot = state["slot"]
        total = jnp.sum(state["total"], axis=0, keepdims=True)
        out = state["out"]
        if again:
            total += sums[slot, :, :] * state["fade"]
            out += acc[slot, :, :] * state["fade"]
        if keep:
            peaks[slot, :, :] = state["peak"]
            sums[slot, :, :] = total
            acc[slot, :, :] = out
        if write:
            out = (out / total).T
            g, r = state["g"], state["r"]
            for h in range(group):
                att[r * block : (r + 1) * block, pl.ds(pl.multiple_of((group * g + h) * HD, HD), HD)] = (
                    out[h * block : (h + 1) * block]
                )

    def sweep(g, runs, again):
        state = prepare(g, 0, runs(0), s_even)
        for piece in state["pieces"]:
            score(state, *piece)
        for r in range(4):
            close(state, again)
            later = prepare(g, r + 1, runs(r + 1), (s_odd, s_even)[r % 2]) if r < 3 else None
            for k in range(max(len(state["pieces"]), len(later["pieces"]) if later else 0)):
                if k < len(state["pieces"]):
                    weigh(state, *state["pieces"][k])
                if later and k < len(later["pieces"]):
                    score(later, *later["pieces"][k])
            finish(state, again, keep=not again or r == 3, write=again)
            state = later

    def from_back():
        states = [
            prepare(g, 3, [(BACK + 8, 2)], (s_even, s_odd)[g % 2].at[pl.ds(g // 2 * 2 * block, 2 * block)])
            for g in range(kv_heads)
        ]
        for stage in (
            lambda s: score(s, *s["pieces"][0]), lambda s: close(s, True),
            lambda s: weigh(s, *s["pieces"][0]), lambda s: finish(s, True, False, True),
        ):
            for state in states:
                stage(state)

    def near_stage(g):
        @pl.when(direct(g))
        def _():
            copy(g, 0, me, near, near).wait_recv()
            near_to_mate(g).start()

        @pl.when(relayed(g))
        def _():
            relay(g).wait_recv()
            near_to_mate(g).start()

    def far_stage(g):
        @pl.when(has_far_prev)
        def _():
            copy(g, 1, me, span(0, 4), span(0, 4)).wait_recv()
            far_to_mate(g).start()

        @pl.when(relaying(g))
        def _():
            relay(g).start()

    def back_late(cond, first):
        for g in range(first, kv_heads):
            pl.when(jnp.logical_and(gives_back, cond))(lambda g=g: to_back(g).start())

    last = kv_heads - 1

    def head_at(step):
        return lax.rem(step + lax.rem(chip, 2), kv_heads)

    from_mate(0).wait_recv()

    @pl.loop(0, kv_heads)
    def _(g):
        sweep(g, own_runs, False)

        @pl.when(g == 0)
        def _():
            pl.when(jnp.logical_and(has_far_next, even))(lambda: to_far(0).start())
            for h in range(1, kv_heads):
                from_mate(h).wait_recv()
                pl.when(has_far_next)(lambda h=h: to_far(h).start())
                pl.when(jnp.logical_and(gives_near(h), odd))(lambda h=h: to_next(h).start())
            pl.when(jnp.logical_and(has_far_next, odd))(lambda: to_far(0).start())

        pl.when(g == last - 1)(lambda: far_stage(head_at(0)))

    @pl.loop(0, kv_heads)
    def _(step):
        g = head_at(step)
        near_stage(g)

        @pl.when(has_prev)
        def _():
            near_from_mate(g).wait_recv()

        @pl.when(jnp.logical_and(core == 1, chip > 1))
        def _():
            far_to_mate(g).wait_recv()

        sweep(g, earlier_runs, True)

        pl.when(step < last)(lambda: far_stage(head_at(step + 1)))
        pl.when(step == 1)(lambda: back_late(even, 0))
        pl.when(step == 2)(lambda: back_late(odd, EARLY))

    def norm(r):
        row = pl.ds(r * block if isinstance(r, int) else pl.multiple_of(r * block, 32), block)
        x = att[row, :]
        mean_square = jnp.mean(x * x, axis=-1, keepdims=True)
        o_ref[row, :] = (x * lax.rsqrt(mean_square + 1e-6) * gain_ref[...]).astype(jnp.bfloat16)

    pl.loop(0, 3)(norm)

    @pl.when(gets_back)
    def _():
        for g in range(kv_heads):
            copy(g, 2, me, span(20, 2), span(20, 2)).wait_recv()
        from_back()

    norm(3)

    for g in range(kv_heads):
        pl.when(gives_near(g))(lambda g=g: to_next(g).wait_send())
        pl.when(relaying(g))(lambda g=g: relay(g).wait_send())
        pl.when(has_far_next)(lambda g=g: to_far(g).wait_send())
        pl.when(gives_back)(lambda g=g: to_back(g).wait_send())
        to_mate(g).wait_send()
        pl.when(has_prev)(lambda g=g: near_to_mate(g).wait_send())
        pl.when(has_far_prev)(lambda g=g: far_to_mate(g).wait_send())


def on_device(n, queries, key_vectors, values, frame_length, frame_reach, out_gain):
    tokens, width = queries.shape
    block = tokens // 4
    kv_heads = key_vectors.shape[1] // HD
    group = width // key_vectors.shape[1]
    anywhere = pl.BlockSpec(memory_space=pl.ANY)
    scalar = pl.BlockSpec(memory_space=pltpu.SMEM)
    return pl.pallas_call(
        functools.partial(kernel, n, block, kv_heads, group),
        out_shape=pltpu.VMEM((tokens, width), jnp.bfloat16),
        in_specs=[anywhere] * 3 + [scalar] * 2 + [pl.BlockSpec(memory_space=pltpu.VMEM)],
        out_specs=pl.BlockSpec(memory_space=pltpu.VMEM),
        scratch_shapes=[
            pltpu.VMEM((kv_heads, 2, SPAN * block, HD), jnp.bfloat16),
            pltpu.VMEM((tokens, width), jnp.bfloat16),
            pltpu.VMEM((12 * block, group * block), jnp.float32),
            pltpu.VMEM((12 * block, group * block), jnp.float32),
            pltpu.VMEM((tokens, width), jnp.float32),
            pltpu.VMEM((4 * kv_heads, HD, group * block), jnp.float32),
            pltpu.VMEM((4 * kv_heads, 1, group * block), jnp.float32),
            pltpu.VMEM((4 * kv_heads, 1, group * block), jnp.float32),
            pltpu.SMEM((4,), jnp.int32),
            pltpu.SMEM((4,), jnp.int32),
            pltpu.SemaphoreType.DMA((kv_heads, 2)),
            pltpu.SemaphoreType.DMA,
            pltpu.SemaphoreType.DMA((kv_heads, 7)),
            pltpu.SemaphoreType.DMA((kv_heads, 7)),
        ],
        compiler_params=pltpu.CompilerParams(
            collective_id=0, has_side_effects=True, vmem_limit_bytes=60 * 1024 * 1024
        ),
    )(queries, key_vectors, values, frame_length, frame_reach, out_gain.reshape(1, width))


def solution(mesh):
    placed = (
        P(("groups", "ctx"), None),
        P(("groups", "ctx"), None),
        P(("groups", "ctx"), None),
        P("groups"),
        P("groups"),
        P(),
    )
    return jax.shard_map(
        functools.partial(on_device, mesh.shape["ctx"]),
        mesh=mesh, in_specs=placed, out_specs=P(("groups", "ctx"), None), check_vma=False,
    )
```

```python
import functools

import jax
import jax.numpy as jnp
from jax import lax
from jax.experimental import pallas as pl
from jax.experimental.pallas import tpu as pltpu
from jax.sharding import PartitionSpec as P

HD = 128
MESH = pl.DeviceIdType.MESH
BACK = 12
SPAN = 22
CHUNK = 512
EARLY = 2


def kernel(
    n, block, kv_heads, group,
    q_hbm, k_hbm, v_hbm, len_ref, reach_ref, gain_ref,
    o_ref,
    kv, qv, s_even, s_odd, att, acc, peaks, sums, lo_ref, up_ref,
    local_sem, q_sem, send_sem, recv_sem,
):
    me = lax.axis_index("ctx")
    chip = lax.div(me, 2)
    core = lax.rem(me, 2)
    chips = n // 2
    mate = 2 * chip + 1 - core
    tokens = 4 * block
    rows = group * block

    has_next = chip < chips - 1
    has_prev = chip > 0
    has_far_next = jnp.logical_and(core == 0, chip < chips - 2)
    has_far_prev = jnp.logical_and(core == 0, chip > 1)
    gives_back = jnp.logical_and(core == 0, has_prev)
    gets_back = jnp.logical_and(core == 1, has_next)
    odd = lax.rem(chip, 2) == 1
    skips = jnp.logical_and(odd, core == 1)
    gets_relay = jnp.logical_and(has_prev, jnp.logical_and(jnp.logical_not(odd), core == 1))
    relays = jnp.logical_and(has_far_prev, odd)
    even = jnp.logical_not(odd)

    def gives_near(g):
        return jnp.logical_and(has_next, jnp.logical_not(jnp.logical_and(skips, g > 0)))

    def relayed(g):
        return jnp.logical_and(gets_relay, g > 0)

    def direct(g):
        return jnp.logical_and(has_prev, jnp.logical_not(relayed(g)))

    def relaying(g):
        return jnp.logical_and(relays, g > 0)

    def span(start, count):
        if isinstance(start, int):
            return pl.ds(start * block, count * block)
        return pl.ds(pl.multiple_of(start * block, 32), count * block)

    own = span(BACK + 4 * core, 4)

    for g in range(kv_heads):
        cols = pl.ds(g * HD, HD)
        pltpu.make_async_copy(k_hbm.at[:, cols], kv.at[g, 0, own, :], local_sem.at[g, 0]).start()
        pltpu.make_async_copy(v_hbm.at[:, cols], kv.at[g, 1, own, :], local_sem.at[g, 1]).start()
    q_copy = pltpu.make_async_copy(q_hbm, qv, q_sem)
    q_copy.start()

    barrier = pltpu.get_barrier_semaphore()

    def greet(cond, target):
        @pl.when(cond)
        def _():
            pl.semaphore_signal(barrier, inc=1, device_id={"ctx": target}, device_id_type=MESH)

        return cond.astype(jnp.int32)

    pl.semaphore_signal(barrier, inc=1, device_id={"ctx": mate}, device_id_type=MESH)
    expected = jnp.int32(1)
    expected += greet(has_next, me + 2)
    expected += greet(has_prev, me - 2)
    expected += greet(has_far_next, me + 4)
    expected += greet(has_far_prev, me - 4)
    expected += greet(gives_back, me - 1)
    expected += greet(gets_back, me + 1)

    def clear(cond, first, count):
        @pl.when(cond)
        def _():
            kv[:, :, first * block : (first + count) * block, :] = jnp.zeros(
                (kv_heads, 2, count * block, HD), jnp.bfloat16
            )

    clear(chip == 0, 0, 12)
    clear(chip == 1, 0, 4)

    pl.semaphore_wait(barrier, expected)

    def copy(g, kind, target, source, dest):
        return pltpu.make_async_remote_copy(
            src_ref=kv.at[g, :, source, :],
            dst_ref=kv.at[g, :, dest, :],
            send_sem=send_sem.at[g, kind],
            recv_sem=recv_sem.at[g, kind],
            device_id={"ctx": target},
            device_id_type=MESH,
        )

    near = span(4 + 4 * core, 4)

    def to_next(g):
        return copy(g, 0, me + 2, own, near)

    def to_far(g):
        return copy(g, 1, me + 4, span(BACK + 4, 4), span(0, 4))

    def to_back(g):
        return copy(g, 2, me - 1, span(BACK, 2), span(20, 2))

    def relay(g):
        return copy(g, 6, me - 1, span(0, 4), span(8, 4))

    def to_mate(g):
        return copy(g, 3, mate, own, own)

    def near_to_mate(g):
        return copy(g, 4, mate, near, near)

    def far_to_mate(g):
        return copy(g, 5, mate, span(3, 1), span(3, 1))

    def from_mate(g):
        theirs = span(BACK + 4 - 4 * core, 4)
        return copy(g, 3, mate, theirs, theirs)

    def near_from_mate(g):
        theirs = span(8 - 4 * core, 4)
        return copy(g, 4, mate, theirs, theirs)

    for g in range(kv_heads):
        cols = pl.ds(g * HD, HD)
        pltpu.make_async_copy(k_hbm.at[:, cols], kv.at[g, 0, own, :], local_sem.at[g, 0]).wait()
        pltpu.make_async_copy(v_hbm.at[:, cols], kv.at[g, 1, own, :], local_sem.at[g, 1]).wait()
        next_now = odd if g == 0 else even
        pl.when(jnp.logical_and(gives_near(g), next_now))(lambda g=g: to_next(g).start())
        to_mate(g).start()
        if g < EARLY:
            pl.when(jnp.logical_and(gives_back, odd))(lambda g=g: to_back(g).start())
    pl.when(jnp.logical_and(gives_near(0), even))(lambda: to_next(0).start())

    first = 8 * chip - BACK

    def ranges(f, carry):
        start = carry[0]
        end = start + len_ref[f]
        low = jnp.maximum(start - reach_ref[f], 0)
        lows, highs = [], []
        for r in range(4):
            c = 4 * me + r
            inside = jnp.logical_and(c >= start, c < end)
            lows.append(jnp.where(inside, low, carry[1][r]))
            highs.append(jnp.where(inside, end, carry[2][r]))
        return end, tuple(lows), tuple(highs)

    zero = jnp.int32(0)
    _, lows, highs = lax.fori_loop(
        0, len_ref.shape[0], ranges, (zero, (zero,) * 4, (zero,) * 4)
    )
    for r in range(4):
        lo_ref[r] = lows[r] - first
        up_ref[r] = highs[r] - first

    factor = 1.4426950408889634 / HD**0.5
    q_copy.wait()

    def fold(x, op):
        return op(x.reshape(x.shape[0] // 8, 8, rows), axis=0)

    def cut(runs):
        places = [start + j for start, count in runs for j in range(count)]
        tall = len(places) * block
        pieces = []
        for top in range(0, tall, CHUNK):
            end = min(top + CHUNK, tall)
            edges = [top] + [b for b in range(0, tall, block) if top < b < end] + [end]
            loads, begin = [], 0
            for start, count in runs:
                a, b = max(top, begin), min(end, begin + count * block)
                if a < b:
                    loads.append((start, a - begin, b - a))
                begin += count * block
            pieces.append((top, end, [(a, b, a // block) for a, b in zip(edges[:-1], edges[1:])], loads))
        return places, pieces

    def own_runs(r):
        return [(BACK, 5)] if r < 2 else [(BACK, 8)]

    def earlier_runs(r):
        return ([((BACK + 5) * core, 3)] if r < 2 else []) + [(3, 9)]

    def prepare(g, r, runs, scores):
        places, pieces = cut(runs)
        low = lo_ref[r]
        up = up_ref[r]

        def load(half, loads):
            found = []
            for start, skip, count in loads:
                where = start * block + skip
                if not isinstance(start, int):
                    where = pl.multiple_of(where, 32)
                found.append(kv[g, half, pl.ds(where, count), :])
            return found[0] if len(found) == 1 else jnp.concatenate(found, axis=0)

        qs = jnp.concatenate(
            [
                qv[r * block : (r + 1) * block, pl.ds(pl.multiple_of((group * g + h) * HD, HD), HD)]
                for h in range(group)
            ],
            axis=0,
        )
        return {
            "best": jnp.full((8, rows), -1e30, jnp.float32),
            "kept": [jnp.logical_and(place >= low, place < up) for place in places],
            "pieces": pieces, "load": load, "qs": qs, "scores": scores,
            "slot": 4 * g + r, "g": g, "r": r,
        }

    def score(state, top, end, parts, loads):
        s = lax.dot_general(
            state["load"](0, loads), state["qs"], (((1,), (1,)), ((), ())),
            preferred_element_type=jnp.float32,
        )
        state["scores"][top:end, :] = s
        for a, b, j in parts:
            peak = fold(s[a - top : b - top], jnp.max)
            state["best"] = jnp.maximum(
                state["best"], jnp.where(state["kept"][j], peak, jnp.float32(-1e30))
            )

    def close(state, again):
        best = jnp.max(state["best"], axis=0, keepdims=True) * factor
        if again:
            before = peaks[state["slot"], :, :]
            best = jnp.maximum(best, before)
            state["fade"] = jnp.exp2(before - best)
        state["peak"] = best
        state["shifts"] = [jnp.where(k, best, jnp.float32(1e30)) for k in state["kept"]]
        state["total"] = jnp.zeros((8, rows), jnp.float32)
        state["out"] = jnp.zeros((HD, rows), jnp.float32)

    def weigh(state, top, end, parts, loads):
        weights = []
        for a, b, j in parts:
            p = jnp.exp2(state["scores"][a:b, :] * factor - state["shifts"][j])
            state["total"] += fold(p, jnp.sum)
            weights.append(p.astype(jnp.bfloat16))
        state["out"] += lax.dot_general(
            state["load"](1, loads), jnp.concatenate(weights, axis=0), (((0,), (0,)), ((), ())),
            preferred_element_type=jnp.float32,
        )

    def finish(state, again, keep, write):
        slot = state["slot"]
        total = jnp.sum(state["total"], axis=0, keepdims=True)
        out = state["out"]
        if again:
            total += sums[slot, :, :] * state["fade"]
            out += acc[slot, :, :] * state["fade"]
        if keep:
            peaks[slot, :, :] = state["peak"]
            sums[slot, :, :] = total
            acc[slot, :, :] = out
        if write:
            out = (out / total).T
            g, r = state["g"], state["r"]
            for h in range(group):
                att[r * block : (r + 1) * block, pl.ds(pl.multiple_of((group * g + h) * HD, HD), HD)] = (
                    out[h * block : (h + 1) * block]
                )

    def norm(r):
        row = pl.ds(r * block if isinstance(r, int) else pl.multiple_of(r * block, 32), block)
        x = att[row, :]
        mean_square = jnp.mean(x * x, axis=-1, keepdims=True)
        o_ref[row, :] = (x * lax.rsqrt(mean_square + 1e-6) * gain_ref[...]).astype(jnp.bfloat16)

    def sweep(g, runs, again, final=False):
        state = prepare(g, 0, runs(0), s_even)
        for piece in state["pieces"]:
            score(state, *piece)
        for r in range(4):
            close(state, again)
            later = prepare(g, r + 1, runs(r + 1), (s_odd, s_even)[r % 2]) if r < 3 else None
            for k in range(max(len(state["pieces"]), len(later["pieces"]) if later else 0)):
                if k < len(state["pieces"]):
                    weigh(state, *state["pieces"][k])
                if later and k < len(later["pieces"]):
                    score(later, *later["pieces"][k])
            finish(state, again, keep=not again or r == 3, write=again)
            if final and r < 3:
                norm(r)
            state = later

    def from_back():
        states = [
            prepare(g, 3, [(BACK + 8, 2)], (s_even, s_odd)[g % 2].at[pl.ds(g // 2 * 2 * block, 2 * block)])
            for g in range(kv_heads)
        ]
        for stage in (
            lambda s: score(s, *s["pieces"][0]), lambda s: close(s, True),
            lambda s: weigh(s, *s["pieces"][0]), lambda s: finish(s, True, False, True),
        ):
            for state in states:
                stage(state)

    def near_stage(g):
        @pl.when(direct(g))
        def _():
            copy(g, 0, me, near, near).wait_recv()
            near_to_mate(g).start()

        @pl.when(relayed(g))
        def _():
            relay(g).wait_recv()
            near_to_mate(g).start()

    def far_stage(g):
        @pl.when(has_far_prev)
        def _():
            copy(g, 1, me, span(0, 4), span(0, 4)).wait_recv()
            far_to_mate(g).start()

        @pl.when(relaying(g))
        def _():
            relay(g).start()

    def back_late(cond, first):
        for g in range(first, kv_heads):
            pl.when(jnp.logical_and(gives_back, cond))(lambda g=g: to_back(g).start())

    last = kv_heads - 1

    def head_at(step):
        return lax.rem(step + lax.rem(chip, 2), kv_heads)

    from_mate(0).wait_recv()

    @pl.loop(0, kv_heads)
    def _(g):
        sweep(g, own_runs, False)

        @pl.when(g == 0)
        def _():
            pl.when(jnp.logical_and(has_far_next, even))(lambda: to_far(0).start())
            for h in range(1, kv_heads):
                from_mate(h).wait_recv()
                pl.when(has_far_next)(lambda h=h: to_far(h).start())
                pl.when(jnp.logical_and(gives_near(h), odd))(lambda h=h: to_next(h).start())
            pl.when(jnp.logical_and(has_far_next, odd))(lambda: to_far(0).start())

        pl.when(g == last - 1)(lambda: far_stage(head_at(0)))

    def arrive(g):
        near_stage(g)

        @pl.when(has_prev)
        def _():
            near_from_mate(g).wait_recv()

        @pl.when(jnp.logical_and(core == 1, chip > 1))
        def _():
            far_to_mate(g).wait_recv()

    @pl.loop(0, last)
    def _(step):
        g = head_at(step)
        arrive(g)
        sweep(g, earlier_runs, True)

        pl.when(step == 2)(lambda: back_late(odd, EARLY))
        far_stage(head_at(step + 1))
        pl.when(step == 1)(lambda: back_late(even, 0))

    arrive(head_at(last))
    sweep(head_at(last), earlier_runs, True, True)

    @pl.when(gets_back)
    def _():
        for g in range(kv_heads):
            copy(g, 2, me, span(20, 2), span(20, 2)).wait_recv()
        from_back()

    norm(3)

    for g in range(kv_heads):
        pl.when(gives_near(g))(lambda g=g: to_next(g).wait_send())
        pl.when(relaying(g))(lambda g=g: relay(g).wait_send())
        pl.when(has_far_next)(lambda g=g: to_far(g).wait_send())
        pl.when(gives_back)(lambda g=g: to_back(g).wait_send())
        to_mate(g).wait_send()
        pl.when(has_prev)(lambda g=g: near_to_mate(g).wait_send())
        pl.when(has_far_prev)(lambda g=g: far_to_mate(g).wait_send())


def on_device(n, queries, key_vectors, values, frame_length, frame_reach, out_gain):
    tokens, width = queries.shape
    block = tokens // 4
    kv_heads = key_vectors.shape[1] // HD
    group = width // key_vectors.shape[1]
    anywhere = pl.BlockSpec(memory_space=pl.ANY)
    scalar = pl.BlockSpec(memory_space=pltpu.SMEM)
    return pl.pallas_call(
        functools.partial(kernel, n, block, kv_heads, group),
        out_shape=pltpu.VMEM((tokens, width), jnp.bfloat16),
        in_specs=[anywhere] * 3 + [scalar] * 2 + [pl.BlockSpec(memory_space=pltpu.VMEM)],
        out_specs=pl.BlockSpec(memory_space=pltpu.VMEM),
        scratch_shapes=[
            pltpu.VMEM((kv_heads, 2, SPAN * block, HD), jnp.bfloat16),
            pltpu.VMEM((tokens, width), jnp.bfloat16),
            pltpu.VMEM((12 * block, group * block), jnp.float32),
            pltpu.VMEM((12 * block, group * block), jnp.float32),
            pltpu.VMEM((tokens, width), jnp.float32),
            pltpu.VMEM((4 * kv_heads, HD, group * block), jnp.float32),
            pltpu.VMEM((4 * kv_heads, 1, group * block), jnp.float32),
            pltpu.VMEM((4 * kv_heads, 1, group * block), jnp.float32),
            pltpu.SMEM((4,), jnp.int32),
            pltpu.SMEM((4,), jnp.int32),
            pltpu.SemaphoreType.DMA((kv_heads, 2)),
            pltpu.SemaphoreType.DMA,
            pltpu.SemaphoreType.DMA((kv_heads, 7)),
            pltpu.SemaphoreType.DMA((kv_heads, 7)),
        ],
        compiler_params=pltpu.CompilerParams(
            collective_id=0, has_side_effects=True, vmem_limit_bytes=60 * 1024 * 1024
        ),
    )(queries, key_vectors, values, frame_length, frame_reach, out_gain.reshape(1, width))


def solution(mesh):
    placed = (
        P(("groups", "ctx"), None),
        P(("groups", "ctx"), None),
        P(("groups", "ctx"), None),
        P("groups"),
        P("groups"),
        P(),
    )
    return jax.shard_map(
        functools.partial(on_device, mesh.shape["ctx"]),
        mesh=mesh, in_specs=placed, out_specs=P(("groups", "ctx"), None), check_vma=False,
    )
```

```python
import functools

import jax
import jax.numpy as jnp
from jax import lax
from jax.experimental import pallas as pl
from jax.experimental.pallas import tpu as pltpu
from jax.sharding import PartitionSpec as P

HD = 128
MESH = pl.DeviceIdType.MESH
BACK = 12
SPAN = 22
CHUNK = 512
EARLY = 2


def kernel(
    n, block, kv_heads, group,
    q_hbm, k_hbm, v_hbm, len_ref, reach_ref, gain_ref,
    o_ref,
    kv, qv, s_even, s_odd, att, acc, peaks, sums, lo_ref, up_ref,
    local_sem, q_sem, send_sem, recv_sem,
):
    me = lax.axis_index("ctx")
    chip = lax.div(me, 2)
    core = lax.rem(me, 2)
    chips = n // 2
    mate = 2 * chip + 1 - core
    tokens = 4 * block
    rows = group * block

    has_next = chip < chips - 1
    has_prev = chip > 0
    has_far_next = jnp.logical_and(core == 0, chip < chips - 2)
    has_far_prev = jnp.logical_and(core == 0, chip > 1)
    gives_back = jnp.logical_and(core == 0, has_prev)
    gets_back = jnp.logical_and(core == 1, has_next)
    odd = lax.rem(chip, 2) == 1
    skips = jnp.logical_and(odd, core == 1)
    gets_relay = jnp.logical_and(has_prev, jnp.logical_and(jnp.logical_not(odd), core == 1))
    relays = jnp.logical_and(has_far_prev, odd)
    even = jnp.logical_not(odd)

    def gives_near(g):
        return jnp.logical_and(has_next, jnp.logical_not(jnp.logical_and(skips, g > 0)))

    def relayed(g):
        return jnp.logical_and(gets_relay, g > 0)

    def direct(g):
        return jnp.logical_and(has_prev, jnp.logical_not(relayed(g)))

    def relaying(g):
        return jnp.logical_and(relays, g > 0)

    def span(start, count):
        if isinstance(start, int):
            return pl.ds(start * block, count * block)
        return pl.ds(pl.multiple_of(start * block, 32), count * block)

    own = span(BACK + 4 * core, 4)

    for g in range(kv_heads):
        cols = pl.ds(g * HD, HD)
        pltpu.make_async_copy(k_hbm.at[:, cols], kv.at[g, 0, own, :], local_sem.at[g, 0]).start()
        pltpu.make_async_copy(v_hbm.at[:, cols], kv.at[g, 1, own, :], local_sem.at[g, 1]).start()
    q_copy = pltpu.make_async_copy(q_hbm, qv, q_sem)
    q_copy.start()

    barrier = pltpu.get_barrier_semaphore()

    def greet(cond, target):
        @pl.when(cond)
        def _():
            pl.semaphore_signal(barrier, inc=1, device_id={"ctx": target}, device_id_type=MESH)

        return cond.astype(jnp.int32)

    pl.semaphore_signal(barrier, inc=1, device_id={"ctx": mate}, device_id_type=MESH)
    expected = jnp.int32(1)
    expected += greet(has_next, me + 2)
    expected += greet(has_prev, me - 2)
    expected += greet(has_far_next, me + 4)
    expected += greet(has_far_prev, me - 4)
    expected += greet(gives_back, me - 1)
    expected += greet(gets_back, me + 1)

    def clear(cond, first, count):
        @pl.when(cond)
        def _():
            kv[:, :, first * block : (first + count) * block, :] = jnp.zeros(
                (kv_heads, 2, count * block, HD), jnp.bfloat16
            )

    clear(chip == 0, 0, 12)
    clear(chip == 1, 0, 4)

    pl.semaphore_wait(barrier, expected)

    def copy(g, kind, target, source, dest):
        return pltpu.make_async_remote_copy(
            src_ref=kv.at[g, :, source, :],
            dst_ref=kv.at[g, :, dest, :],
            send_sem=send_sem.at[g, kind],
            recv_sem=recv_sem.at[g, kind],
            device_id={"ctx": target},
            device_id_type=MESH,
        )

    near = span(4 + 4 * core, 4)

    def to_next(g):
        return copy(g, 0, me + 2, own, near)

    def to_far(g):
        return copy(g, 1, me + 4, span(BACK + 4, 4), span(0, 4))

    def to_back(g):
        return copy(g, 2, me - 1, span(BACK, 2), span(20, 2))

    def relay(g):
        return copy(g, 6, me - 1, span(0, 4), span(8, 4))

    def to_mate(g):
        return copy(g, 3, mate, own, own)

    def near_to_mate(g):
        return copy(g, 4, mate, near, near)

    def far_to_mate(g):
        return copy(g, 5, mate, span(3, 1), span(3, 1))

    def from_mate(g):
        theirs = span(BACK + 4 - 4 * core, 4)
        return copy(g, 3, mate, theirs, theirs)

    def near_from_mate(g):
        theirs = span(8 - 4 * core, 4)
        return copy(g, 4, mate, theirs, theirs)

    for g in range(kv_heads):
        cols = pl.ds(g * HD, HD)
        pltpu.make_async_copy(k_hbm.at[:, cols], kv.at[g, 0, own, :], local_sem.at[g, 0]).wait()
        pltpu.make_async_copy(v_hbm.at[:, cols], kv.at[g, 1, own, :], local_sem.at[g, 1]).wait()
        next_now = odd if g == 0 else even
        pl.when(jnp.logical_and(gives_near(g), next_now))(lambda g=g: to_next(g).start())
        to_mate(g).start()
        if g < EARLY:
            pl.when(jnp.logical_and(gives_back, odd))(lambda g=g: to_back(g).start())
    pl.when(jnp.logical_and(gives_near(0), even))(lambda: to_next(0).start())

    first = 8 * chip - BACK

    def ranges(f, carry):
        start = carry[0]
        end = start + len_ref[f]
        low = jnp.maximum(start - reach_ref[f], 0)
        lows, highs = [], []
        for r in range(4):
            c = 4 * me + r
            inside = jnp.logical_and(c >= start, c < end)
            lows.append(jnp.where(inside, low, carry[1][r]))
            highs.append(jnp.where(inside, end, carry[2][r]))
        return end, tuple(lows), tuple(highs)

    zero = jnp.int32(0)
    _, lows, highs = lax.fori_loop(
        0, len_ref.shape[0], ranges, (zero, (zero,) * 4, (zero,) * 4)
    )
    for r in range(4):
        lo_ref[r] = lows[r] - first
        up_ref[r] = highs[r] - first

    factor = 1.4426950408889634 / HD**0.5
    q_copy.wait()

    def fold(x, op):
        return op(x.reshape(x.shape[0] // 8, 8, rows), axis=0)

    def cut(runs):
        places = [start + j for start, count in runs for j in range(count)]
        tall = len(places) * block
        pieces = []
        for top in range(0, tall, CHUNK):
            end = min(top + CHUNK, tall)
            edges = [top] + [b for b in range(0, tall, block) if top < b < end] + [end]
            loads, begin = [], 0
            for start, count in runs:
                a, b = max(top, begin), min(end, begin + count * block)
                if a < b:
                    loads.append((start, a - begin, b - a))
                begin += count * block
            pieces.append((top, end, [(a, b, a // block) for a, b in zip(edges[:-1], edges[1:])], loads))
        return places, pieces

    def own_runs(r):
        return [(BACK, 5)] if r < 2 else [(BACK, 8)]

    def earlier_runs(r):
        return ([((BACK + 5) * core, 3)] if r < 2 else []) + [(3, 9)]

    def prepare(g, r, runs, scores):
        places, pieces = cut(runs)
        low = lo_ref[r]
        up = up_ref[r]

        def load(half, loads):
            found = []
            for start, skip, count in loads:
                where = start * block + skip
                if not isinstance(start, int):
                    where = pl.multiple_of(where, 32)
                found.append(kv[g, half, pl.ds(where, count), :])
            return found[0] if len(found) == 1 else jnp.concatenate(found, axis=0)

        qs = jnp.concatenate(
            [
                qv[r * block : (r + 1) * block, pl.ds(pl.multiple_of((group * g + h) * HD, HD), HD)]
                for h in range(group)
            ],
            axis=0,
        )
        return {
            "best": jnp.full((8, rows), -1e30, jnp.float32),
            "kept": [jnp.logical_and(place >= low, place < up) for place in places],
            "pieces": pieces, "load": load, "qs": qs, "scores": scores,
            "slot": 4 * g + r, "g": g, "r": r,
        }

    def score(state, top, end, parts, loads):
        s = lax.dot_general(
            state["load"](0, loads), state["qs"], (((1,), (1,)), ((), ())),
            preferred_element_type=jnp.float32,
        )
        state["scores"][top:end, :] = s
        for a, b, j in parts:
            peak = fold(s[a - top : b - top], jnp.max)
            state["best"] = jnp.maximum(
                state["best"], jnp.where(state["kept"][j], peak, jnp.float32(-1e30))
            )

    def close(state, again):
        best = jnp.max(state["best"], axis=0, keepdims=True) * factor
        if again:
            before = peaks[state["slot"], :, :]
            best = jnp.maximum(best, before)
            state["fade"] = jnp.exp2(before - best)
        state["peak"] = best
        state["shifts"] = [jnp.where(k, best, jnp.float32(1e30)) for k in state["kept"]]
        state["total"] = jnp.zeros((8, rows), jnp.float32)
        state["out"] = jnp.zeros((HD, rows), jnp.float32)

    def weigh(state, top, end, parts, loads):
        weights = []
        for a, b, j in parts:
            p = jnp.exp2(state["scores"][a:b, :] * factor - state["shifts"][j])
            state["total"] += fold(p, jnp.sum)
            weights.append(p.astype(jnp.bfloat16))
        state["out"] += lax.dot_general(
            state["load"](1, loads), jnp.concatenate(weights, axis=0), (((0,), (0,)), ((), ())),
            preferred_element_type=jnp.float32,
        )

    def finish(state, again, keep, write):
        slot = state["slot"]
        total = jnp.sum(state["total"], axis=0, keepdims=True)
        out = state["out"]
        if again:
            total += sums[slot, :, :] * state["fade"]
            out += acc[slot, :, :] * state["fade"]
        if keep:
            peaks[slot, :, :] = state["peak"]
            sums[slot, :, :] = total
            acc[slot, :, :] = out
        if write:
            out = (out / total).T
            g, r = state["g"], state["r"]
            for h in range(group):
                att[r * block : (r + 1) * block, pl.ds(pl.multiple_of((group * g + h) * HD, HD), HD)] = (
                    out[h * block : (h + 1) * block]
                )

    def norm(r):
        row = pl.ds(r * block if isinstance(r, int) else pl.multiple_of(r * block, 32), block)
        x = att[row, :]
        mean_square = jnp.mean(x * x, axis=-1, keepdims=True)
        o_ref[row, :] = (x * lax.rsqrt(mean_square + 1e-6) * gain_ref[...]).astype(jnp.bfloat16)

    def sweep(g, runs, again, final=False):
        state = prepare(g, 0, runs(0), s_even)
        for piece in state["pieces"]:
            score(state, *piece)
        for r in range(4):
            close(state, again)
            later = prepare(g, r + 1, runs(r + 1), (s_odd, s_even)[r % 2]) if r < 3 else None
            for k in range(max(len(state["pieces"]), len(later["pieces"]) if later else 0)):
                if k < len(state["pieces"]):
                    weigh(state, *state["pieces"][k])
                if later and k < len(later["pieces"]):
                    score(later, *later["pieces"][k])
            finish(state, again, keep=not again or r == 3, write=again)
            if final and r < 3:
                norm(r)
            state = later

    def from_back():
        states = [
            prepare(g, 3, [(BACK + 8, 2)], (s_even, s_odd)[g % 2].at[pl.ds(g // 2 * 2 * block, 2 * block)])
            for g in range(kv_heads)
        ]
        for stage in (
            lambda s: score(s, *s["pieces"][0]), lambda s: close(s, True),
            lambda s: weigh(s, *s["pieces"][0]), lambda s: finish(s, True, False, True),
        ):
            for state in states:
                stage(state)

    def near_stage(g):
        @pl.when(direct(g))
        def _():
            copy(g, 0, me, near, near).wait_recv()
            near_to_mate(g).start()

        @pl.when(relayed(g))
        def _():
            relay(g).wait_recv()
            near_to_mate(g).start()

    def far_stage(g):
        @pl.when(has_far_prev)
        def _():
            copy(g, 1, me, span(0, 4), span(0, 4)).wait_recv()
            far_to_mate(g).start()

        @pl.when(relaying(g))
        def _():
            relay(g).start()

    def back_late(cond, first):
        for g in range(first, kv_heads):
            pl.when(jnp.logical_and(gives_back, cond))(lambda g=g: to_back(g).start())

    last = kv_heads - 1

    def head_at(step):
        return lax.rem(step + lax.rem(chip, 2), kv_heads)

    from_mate(0).wait_recv()

    @pl.loop(0, kv_heads)
    def _(g):
        sweep(g, own_runs, False)

        @pl.when(g == 0)
        def _():
            pl.when(jnp.logical_and(has_far_next, even))(lambda: to_far(0).start())
            for h in range(1, kv_heads):
                from_mate(h).wait_recv()
                pl.when(has_far_next)(lambda h=h: to_far(h).start())
                pl.when(jnp.logical_and(gives_near(h), odd))(lambda h=h: to_next(h).start())
            pl.when(jnp.logical_and(has_far_next, odd))(lambda: to_far(0).start())

        pl.when(g == last - 1)(lambda: far_stage(head_at(0)))

    def arrive(g):
        near_stage(g)

        @pl.when(has_prev)
        def _():
            near_from_mate(g).wait_recv()

        @pl.when(jnp.logical_and(core == 1, chip > 1))
        def _():
            far_to_mate(g).wait_recv()

    @pl.loop(0, last)
    def _(step):
        g = head_at(step)
        arrive(g)
        pl.when(step == 2)(lambda: back_late(odd, EARLY))
        sweep(g, earlier_runs, True)

        far_stage(head_at(step + 1))
        pl.when(step == 1)(lambda: back_late(even, 0))

    arrive(head_at(last))
    sweep(head_at(last), earlier_runs, True, True)

    @pl.when(gets_back)
    def _():
        for g in range(kv_heads):
            copy(g, 2, me, span(20, 2), span(20, 2)).wait_recv()
        from_back()

    norm(3)

    for g in range(kv_heads):
        pl.when(gives_near(g))(lambda g=g: to_next(g).wait_send())
        pl.when(relaying(g))(lambda g=g: relay(g).wait_send())
        pl.when(has_far_next)(lambda g=g: to_far(g).wait_send())
        pl.when(gives_back)(lambda g=g: to_back(g).wait_send())
        to_mate(g).wait_send()
        pl.when(has_prev)(lambda g=g: near_to_mate(g).wait_send())
        pl.when(has_far_prev)(lambda g=g: far_to_mate(g).wait_send())


def on_device(n, queries, key_vectors, values, frame_length, frame_reach, out_gain):
    tokens, width = queries.shape
    block = tokens // 4
    kv_heads = key_vectors.shape[1] // HD
    group = width // key_vectors.shape[1]
    anywhere = pl.BlockSpec(memory_space=pl.ANY)
    scalar = pl.BlockSpec(memory_space=pltpu.SMEM)
    return pl.pallas_call(
        functools.partial(kernel, n, block, kv_heads, group),
        out_shape=pltpu.VMEM((tokens, width), jnp.bfloat16),
        in_specs=[anywhere] * 3 + [scalar] * 2 + [pl.BlockSpec(memory_space=pltpu.VMEM)],
        out_specs=pl.BlockSpec(memory_space=pltpu.VMEM),
        scratch_shapes=[
            pltpu.VMEM((kv_heads, 2, SPAN * block, HD), jnp.bfloat16),
            pltpu.VMEM((tokens, width), jnp.bfloat16),
            pltpu.VMEM((12 * block, group * block), jnp.float32),
            pltpu.VMEM((12 * block, group * block), jnp.float32),
            pltpu.VMEM((tokens, width), jnp.float32),
            pltpu.VMEM((4 * kv_heads, HD, group * block), jnp.float32),
            pltpu.VMEM((4 * kv_heads, 1, group * block), jnp.float32),
            pltpu.VMEM((4 * kv_heads, 1, group * block), jnp.float32),
            pltpu.SMEM((4,), jnp.int32),
            pltpu.SMEM((4,), jnp.int32),
            pltpu.SemaphoreType.DMA((kv_heads, 2)),
            pltpu.SemaphoreType.DMA,
            pltpu.SemaphoreType.DMA((kv_heads, 7)),
            pltpu.SemaphoreType.DMA((kv_heads, 7)),
        ],
        compiler_params=pltpu.CompilerParams(
            collective_id=0, has_side_effects=True, vmem_limit_bytes=60 * 1024 * 1024
        ),
    )(queries, key_vectors, values, frame_length, frame_reach, out_gain.reshape(1, width))


def solution(mesh):
    placed = (
        P(("groups", "ctx"), None),
        P(("groups", "ctx"), None),
        P(("groups", "ctx"), None),
        P("groups"),
        P("groups"),
        P(),
    )
    return jax.shard_map(
        functools.partial(on_device, mesh.shape["ctx"]),
        mesh=mesh, in_specs=placed, out_specs=P(("groups", "ctx"), None), check_vma=False,
    )
```
